32 devices in a mesh: section: 4 (over x, core), ha: 2 (over y), wa: 4 (over z).
Axes of the slice: x: 2, y: 2, z: 4, core: 2. Of those that a mesh axis runs over, the one named last changes fastest.
Arguments:
- queries: bfloat16 [4, 4, 4, 8, 16, 2560], P('section', None, 'ha', 'wa'), may hold values from -28 to 28
- keys_values: bfloat16 [2, 4, 4, 4, 8, 16, 2560], P(None, 'section', None, 'ha', 'wa'), may hold values from -28 to 28
- grad_out: bfloat16 [4, 4, 4, 8, 16, 2560], P('section', None, 'ha', 'wa'), may hold values from -6 to 6
- time_start: int32 [4, 4, 8], P(None, 'ha', 'wa'), may hold values from 0 to 1, as said below
Outputs:
- grad_qkv: bfloat16 [3, 4, 4, 4, 8, 16, 2560], P(None, 'section', None, 'ha', 'wa')
The draws below stay inside these ranges and needn't reach their ends.
Inputs may be any that keep to these rules, and one draw needn't show every extreme that they name: Each tile's window begins at most two tiles before the tile and never after it: max(0, t - 2) <= time_start[t, h, w] <= min(t, 1) for time index t.
All inputs are finite; a program needn't handle non-finite values.
Results may differ from the reference program's by a relative error of at most 0.012.
Values may be sent and summed in bfloat16 or wider, within the bound.
A program may use at most 192 MiB of HBM per device.

```python
import jax
import jax.numpy as jnp
from jax import lax

HEADS = 20
HEAD_DIM = 128
GT = 4
HT = 2
WT = 2
SECTIONS = 4
GH = 4
GW = 8
TILE_TOK = 16
CHANNELS = 2560
N_HA = 2
N_WA = 4


def drawn_draw(key):
    base = jax.random.fold_in(key, 71)
    pair_shape = (2, SECTIONS, GT, GH, GW, TILE_TOK, CHANNELS)
    pairs = jnp.clip(jax.random.normal(jax.random.fold_in(base, 1), pair_shape, jnp.float32), -6.0, 6.0)
    queries = jnp.clip(jax.random.normal(jax.random.fold_in(base, 2), pair_shape[1:], jnp.float32), -6.0, 6.0)
    return (queries, pairs)


def draw_queries(key, part):
    return drawn_draw(key)[0].astype(jnp.bfloat16)


def draw_keys_values(key, part):
    return drawn_draw(key)[1].astype(jnp.bfloat16)


def draw_time_start(key, part):
    shifts = jax.random.randint(jax.random.fold_in(key, 5), (GT, GH, GW), 0, 3)
    tiles = jnp.arange(GT, dtype=jnp.int32)[:, None, None]
    return jnp.clip(tiles - shifts, 0, GT - 3).astype(jnp.int32)


def block_levels(own_key, shape, split, low, largest):
    factor_of = 1.0
    for axis_at, blocks in split:
        steps = jax.random.uniform(jax.random.fold_in(jax.random.fold_in(own_key, 6), axis_at), (blocks,), jnp.float32, low / len(split), largest / len(split))
        factor_of = factor_of * jnp.repeat(jnp.exp(steps), shape[axis_at] // blocks).reshape((-1,) + (1,) * (len(shape) - 1 - axis_at))
    return factor_of


def centred(stream_key, dims, deviation, limit, shards=(), held_as=jnp.bfloat16):
    loudness = block_levels(stream_key, dims, shards, -0.22, 0.18) if shards else 1.0
    array = jax.random.normal(stream_key, dims, jnp.float32) * deviation * loudness
    return jnp.minimum(jnp.maximum(array, -limit), limit).astype(held_as)


def setup_inputs(seed: int = 0) -> dict:
    splits = jax.random.split(jax.random.key(seed), 5)
    queries = draw_queries(jax.random.fold_in(splits[4], 71), 0)
    keys_values = draw_keys_values(jax.random.fold_in(splits[4], 71), 0)
    grad_out = centred(splits[2], (SECTIONS, GT, GH, GW, TILE_TOK, CHANNELS), 1.0, 6.0, ((0, 4), (2, 2), (3, 4)))
    time_start = draw_time_start(jax.random.fold_in(splits[4], 71), 0)
    return {"queries": queries, "keys_values": keys_values, "grad_out": grad_out, "time_start": time_start}


def tile_grads(query_block, pair_block, grad_block, starts, tile_tok):
    scale_factor = HEAD_DIM ** -0.5
    query_full = query_block.astype(jnp.float32)
    key_part = pair_block[0].astype(jnp.float32)
    value_part = pair_block[1].astype(jnp.float32)
    grad_full = grad_block.astype(jnp.float32)
    scores = jnp.einsum("qhd,khd->hqk", query_full, key_part) * scale_factor
    key_tile = jnp.arange(key_part.shape[0], dtype=jnp.int32) // (9 * tile_tok)
    window_low = jnp.repeat(starts.astype(jnp.int32), tile_tok)
    inside = (key_tile[None, :] >= window_low[:, None]) & (key_tile[None, :] < window_low[:, None] + 3)
    scores = jnp.where(inside[None], scores, -jnp.inf)
    maximum = jnp.max(scores, axis=-1, keepdims=True)
    weights = jnp.exp(scores - maximum)
    softmax_out = weights / jnp.sum(weights, axis=-1, keepdims=True)
    weights_low = softmax_out.astype(jnp.bfloat16).astype(jnp.float32)
    grad_probs = jnp.einsum("qhd,khd->hqk", grad_full, value_part)
    row_delta = jnp.sum(softmax_out * grad_probs, axis=-1, keepdims=True)
    grad_scores = (softmax_out * (grad_probs - row_delta)).astype(jnp.bfloat16).astype(jnp.float32)
    query_grad = jnp.einsum("hqk,khd->qhd", grad_scores, key_part) * scale_factor
    key_grad = jnp.einsum("hqk,qhd->khd", grad_scores, query_full) * scale_factor
    value_grad = jnp.einsum("hqk,qhd->khd", weights_low, grad_full)
    return query_grad, jnp.stack([key_grad, value_grad])


def reference(queries, keys_values, grad_out, time_start):
    tile_count = GT * TILE_TOK
    interior = jnp.zeros((HT + 2, WT + 2), dtype=bool).at[1:HT + 1, 1:WT + 1].set(True)

    def section_grads(operands):
        section_queries, section_pairs, section_grads_out = operands
        total = jnp.zeros((2, GT, GH + 2, GW + 2, TILE_TOK, CHANNELS), jnp.float32)
        query_total = jnp.zeros((GT, GH, GW, TILE_TOK, CHANNELS), jnp.bfloat16)
        for dev_row in range(N_HA):
            for dev_col in range(N_WA):
                partial_value = jnp.zeros((2, GT, HT + 2, WT + 2, TILE_TOK, CHANNELS), jnp.float32)
                for tile_row in range(HT):
                    for tile_col in range(WT):
                        glob_row = dev_row * HT + tile_row
                        glob_col = dev_col * WT + tile_col
                        top_start = min(max(glob_row - 1, 0), GH - 3)
                        left_start = min(max(glob_col - 1, 0), GW - 3)
                        window = section_pairs[:, :, top_start:top_start + 3, left_start:left_start + 3]
                        pair_block = window.reshape(2, tile_count * 9, HEADS, HEAD_DIM)
                        query_block = section_queries[:, glob_row, glob_col].reshape(tile_count, HEADS, HEAD_DIM)
                        grad_block = section_grads_out[:, glob_row, glob_col].reshape(tile_count, HEADS, HEAD_DIM)
                        query_grad, pair_grad = tile_grads(query_block, pair_block, grad_block, time_start[:, glob_row, glob_col], TILE_TOK)
                        query_total = query_total.at[:, glob_row, glob_col].set(query_grad.reshape(GT, TILE_TOK, CHANNELS).astype(jnp.bfloat16))
                        ext_row = top_start - dev_row * HT + 1
                        ext_col = left_start - dev_col * WT + 1
                        partial_value = partial_value.at[:, :, ext_row:ext_row + 3, ext_col:ext_col + 3].add(pair_grad.reshape(2, GT, 3, 3, TILE_TOK, CHANNELS))
                rim_values = lax.optimization_barrier(partial_value.astype(jnp.bfloat16)).astype(jnp.float32)
                mixed = jnp.where(interior[None, None, :, :, None, None], partial_value, rim_values)
                total = total.at[:, :, dev_row * HT:dev_row * HT + HT + 2, dev_col * WT:dev_col * WT + WT + 2].add(mixed)
        pair_total = total[:, :, 1:GH + 1, 1:GW + 1].astype(jnp.bfloat16)
        return jnp.concatenate([query_total[None], pair_total], axis=0)

    per_section = lax.map(section_grads, (queries, jnp.moveaxis(keys_values, 1, 0), grad_out))
    shifted = jnp.roll(per_section, -1, axis=0)
    return jnp.moveaxis(shifted, 0, 1)
```

```python
import functools

import jax
import jax.numpy as jnp
from jax import lax
from jax.experimental import pallas as pl
from jax.experimental.pallas import tpu as pltpu
from jax.sharding import PartitionSpec as P

HEAD_DIM = 128
HEADS_PER_CHUNK = 2
MESH = pl.DeviceIdType.MESH
F32 = jnp.float32
BF16 = jnp.bfloat16

Y_KV, Z_KV, Z_CORNER, Z_PART, Y_PART, OUT_Q, OUT_KV, KINDS = 0, 1, 3, 5, 7, 8, 9, 10


def dot(a, b, contract):
    return lax.dot_general(a, b, ((contract[0], contract[1]), ((), ())), preferred_element_type=F32)


def kernel(sizes, starts, q, kv, go, out, hy, hz, pz_send, pz_recv, py_send, py_recv,
           acc, acc_y, dq, dkv, bias, send_sem, recv_sem):
    n_sec, n_ha, n_wa, chunks, width = sizes
    grid_t, rows, cols, tok, _ = q.shape
    sec, ha, wa = lax.axis_index("section"), lax.axis_index("ha"), lax.axis_index("wa")
    before = lax.rem(sec + n_sec - 1, n_sec)
    after = lax.rem(sec + 1, n_sec)
    other = 1 - ha
    edge = other * (rows - 1)
    has = (wa > 0, wa < n_wa - 1)
    peer = (wa - 1, wa + 1)
    near = (0, cols - 1)
    scale = HEAD_DIM ** (-0.5)

    barrier = pltpu.get_barrier_semaphore()
    pl.semaphore_signal(barrier, inc=1, device_id=(before, ha, wa), device_id_type=MESH)
    pl.semaphore_signal(barrier, inc=1, device_id=(after, ha, wa), device_id_type=MESH)
    pl.semaphore_signal(barrier, inc=1, device_id=(sec, other, wa), device_id_type=MESH)
    for side in (0, 1):
        @pl.when(has[side])
        def _():
            pl.semaphore_signal(barrier, inc=1, device_id=(sec, ha, peer[side]), device_id_type=MESH)
    pl.semaphore_wait(barrier, 3 + jnp.minimum(wa, 1) + jnp.minimum(n_wa - 1 - wa, 1))

    def lanes(c):
        return pl.ds(pl.multiple_of(c * width, width), width)

    def remote(src, dst, sent, arrived, c, device):
        return pltpu.make_async_remote_copy(
            src_ref=src, dst_ref=dst, send_sem=send_sem.at[sent, c], recv_sem=recv_sem.at[arrived, c],
            device_id=device, device_id_type=MESH)

    def y_kv(c):
        return remote(kv.at[:, :, edge, :, :, lanes(c)], hy.at[:, :, :, :, lanes(c)],
                      Y_KV, Y_KV, c, (sec, other, wa))

    def z_kv(side, c):
        return remote(kv.at[:, :, :, near[side], :, lanes(c)], hz.at[1 - side, :, :, 0:rows, :, lanes(c)],
                      Z_KV + side, Z_KV + 1 - side, c, (sec, ha, peer[side]))

    def z_corner(side, c):
        return remote(hy.at[:, :, near[side], :, lanes(c)], hz.at[1 - side, :, :, rows, :, lanes(c)],
                      Z_CORNER + side, Z_CORNER + 1 - side, c, (sec, ha, peer[side]))

    def z_part(side, c):
        return remote(pz_send.at[side, :, :, :, :, lanes(c)], pz_recv.at[1 - side, :, :, :, :, lanes(c)],
                      Z_PART + side, Z_PART + 1 - side, c, (sec, ha, peer[side]))

    def y_part(c):
        return remote(py_send.at[:, :, :, :, lanes(c)], py_recv.at[:, :, :, :, lanes(c)],
                      Y_PART, Y_PART, c, (sec, other, wa))

    def out_q(c):
        return remote(dq.at[:, :, :, :, lanes(c)], out.at[0, :, :, :, :, lanes(c)],
                      OUT_Q, OUT_Q, c, (before, ha, wa))

    def out_kv(c):
        return remote(dkv.at[:, :, :, :, :, lanes(c)], out.at[pl.ds(1, 2), :, :, :, :, lanes(c)],
                      OUT_KV, OUT_KV, c, (before, ha, wa))

    n_own, n_y, n_z = grid_t * rows * cols * tok, grid_t * cols * tok, grid_t * (rows + 1) * tok
    n_q = n_own
    cut = (0, n_own, n_own + n_y, n_own + n_y + n_z, n_own + n_y + 2 * n_z)

    def stage_send(c):
        y_kv(c).start()
        for side in (0, 1):
            @pl.when(has[side])
            def _():
                z_kv(side, c).start()

    def stage_corner(c):
        y_kv(c).wait_recv()
        for side in (0, 1):
            @pl.when(has[side])
            def _():
                z_corner(side, c).start()

    def head(h):
        ch = pl.ds(pl.multiple_of(h * HEAD_DIM, HEAD_DIM), HEAD_DIM)
        qh = q[:, :, :, :, ch].reshape(n_q, HEAD_DIM)
        gh = go[:, :, :, :, ch].reshape(n_q, HEAD_DIM)

        def gather(i):
            return jnp.concatenate([
                kv[i, :, :, :, :, ch].reshape(n_own, HEAD_DIM), hy[i, :, :, :, ch].reshape(n_y, HEAD_DIM),
                hz[0, i, :, :, :, ch].reshape(n_z, HEAD_DIM), hz[1, i, :, :, :, ch].reshape(n_z, HEAD_DIM)])

        k, v = gather(0), gather(1)
        s = dot(k, qh, ((1,), (1,))) * scale + bias[...]
        e = jnp.exp(s - jnp.max(s, axis=0, keepdims=True))
        p = e * (1.0 / jnp.sum(e, axis=0, keepdims=True))
        dp = dot(v, gh, ((1,), (1,)))
        delta = jnp.sum(p * dp, axis=0, keepdims=True)
        ds = (p * (dp - delta)).astype(BF16)
        grads = (dot(ds, qh, ((1,), (0,))) * scale, dot(p.astype(BF16), gh, ((1,), (0,))))
        q_grad = dot(ds, k, ((0,), (0,))) * scale
        dq[:, :, :, :, ch] = q_grad.astype(BF16).reshape(grid_t, rows, cols, tok, HEAD_DIM)
        for i in (0, 1):
            acc[i, :, :, :, :, ch] = grads[i][cut[0]:cut[1]].reshape(grid_t, rows, cols, tok, HEAD_DIM)
            acc_y[i, :, :, :, ch] = grads[i][cut[1]:cut[2]].reshape(grid_t, cols, tok, HEAD_DIM)
            for side in (0, 1):
                part = grads[i][cut[2 + side]:cut[3 + side]].astype(BF16)
                pz_send[side, i, :, :, :, ch] = part.reshape(grid_t, rows + 1, tok, HEAD_DIM)

    def stage_compute(c):
        for side in (0, 1):
            @pl.when(has[side])
            def _():
                arrived_z(side, c)
        for j in range(HEADS_PER_CHUNK):
            head(c * HEADS_PER_CHUNK + j)
        for side in (0, 1):
            @pl.when(has[side])
            def _():
                z_part(side, c).start()
        out_q(c).start()

    def arrived_z(side, c):
        z_kv(1 - side, c).wait_recv()
        z_corner(1 - side, c).wait_recv()

    def stage_fold(c):
        ch = lanes(c)
        for side in (0, 1):
            @pl.when(has[side])
            def _():
                z_part(1 - side, c).wait_recv()
                for i in (0, 1):
                    acc[i, :, :, near[side], :, ch] += pz_recv[side, i, :, 0:rows, :, ch].astype(F32)
                    acc_y[i, :, near[side], :, ch] += pz_recv[side, i, :, rows, :, ch].astype(F32)
        py_send[:, :, :, :, ch] = acc_y[:, :, :, :, ch].astype(BF16)
        y_part(c).start()

    def stage_out(c):
        ch = lanes(c)
        y_part(c).wait_recv()
        acc[:, :, edge, :, :, ch] += py_recv[:, :, :, :, ch].astype(F32)
        dkv[:, :, :, :, :, ch] = acc[:, :, :, :, :, ch].astype(BF16)
        out_kv(c).start()

    stage_send(0)
    stage_send(1)

    lane = lax.broadcasted_iota(jnp.int32, (1, n_q), 1)
    first = jnp.zeros((1, n_q), jnp.int32)
    for t in range(grid_t):
        for r in range(rows):
            for c in range(cols):
                tile = (t * rows + r) * cols + c
                first = jnp.where(lane // tok == tile, starts[t, r, c], first)
    col = (lane // tok) % cols
    low_first, high_last = wa == 0, wa == n_wa - 1
    in_left = jnp.where(low_first, 0, jnp.where(high_last, 1, (col == 0).astype(jnp.int32)))
    in_right = jnp.where(high_last, 0, jnp.where(low_first, 1, (col == cols - 1).astype(jnp.int32)))
    always = jnp.ones((1, n_q), jnp.int32)
    for at, per_t, inside in ((0, rows * cols * tok, always), (1, cols * tok, always),
                              (2, (rows + 1) * tok, in_left), (3, (rows + 1) * tok, in_right)):
        for t in range(grid_t):
            seen = (first <= t) & (first + 2 >= t) & (inside > 0)
            row = jnp.where(seen, 0.0, -1e30).astype(F32)
            bias[cut[at] + t * per_t:cut[at] + (t + 1) * per_t, :] = jnp.broadcast_to(row, (per_t, n_q))
    for side in (0, 1):
        @pl.when(jnp.logical_not(has[side]))
        def _():
            hz[side] = jnp.zeros(hz.shape[1:], BF16)

    def step(i, carry):
        @pl.when(i + 2 < chunks)
        def _():
            stage_send(i + 2)

        @pl.when(i + 1 < chunks)
        def _():
            stage_corner(i + 1)

        @pl.when(i < chunks)
        def _():
            stage_compute(i)

        @pl.when((i >= 1) & (i < chunks + 1))
        def _():
            stage_fold(i - 1)

        @pl.when(i >= 2)
        def _():
            stage_out(i - 2)
        return carry

    stage_corner(0)
    lax.fori_loop(0, chunks + 2, step, 0)

    def finish(c, carry):
        y_kv(c).wait_send()
        y_part(c).wait_send()
        for side in (0, 1):
            @pl.when(has[side])
            def _():
                z_kv(side, c).wait_send()
                z_corner(side, c).wait_send()
                z_part(side, c).wait_send()
        out_q(c).wait()
        out_kv(c).wait()
        return carry

    lax.fori_loop(0, chunks, finish, 0)


def local(mesh_sizes, queries, keys_values, grad_out, time_start):
    n_sec, n_ha, n_wa = mesh_sizes
    q, kv, go = queries[0], keys_values[:, 0], grad_out[0]
    grid_t, rows, cols, tok, channels = q.shape
    assert n_ha == 2 and rows == 2 and cols == 2 and n_wa >= 2 and n_sec >= 2
    width = HEADS_PER_CHUNK * HEAD_DIM
    assert channels % width == 0
    chunks = channels // width
    assert chunks >= 2
    n_q = grid_t * rows * cols * tok
    n_k = n_q + grid_t * tok * (cols + 2 * (rows + 1))
    vmem = pl.BlockSpec(memory_space=pltpu.VMEM)
    out = pl.pallas_call(
        functools.partial(kernel, (n_sec, n_ha, n_wa, chunks, width)),
        out_shape=jax.ShapeDtypeStruct((3,) + q.shape, BF16),
        in_specs=[pl.BlockSpec(memory_space=pltpu.SMEM), vmem, vmem, vmem],
        out_specs=pl.BlockSpec(memory_space=pl.ANY),
        scratch_shapes=[
            pltpu.VMEM((2, grid_t, cols, tok, channels), BF16),
            pltpu.VMEM((2, 2, grid_t, rows + 1, tok, channels), BF16),
            pltpu.VMEM((2, 2, grid_t, rows + 1, tok, channels), BF16),
            pltpu.VMEM((2, 2, grid_t, rows + 1, tok, channels), BF16),
            pltpu.VMEM((2, grid_t, cols, tok, channels), BF16),
            pltpu.VMEM((2, grid_t, cols, tok, channels), BF16),
            pltpu.VMEM((2,) + q.shape, F32),
            pltpu.VMEM((2, grid_t, cols, tok, channels), F32),
            pltpu.VMEM(q.shape, BF16),
            pltpu.VMEM((2,) + q.shape, BF16),
            pltpu.VMEM((n_k, n_q), F32),
            pltpu.SemaphoreType.DMA((KINDS, chunks)),
            pltpu.SemaphoreType.DMA((KINDS, chunks)),
        ],
        compiler_params=pltpu.CompilerParams(
            collective_id=0, has_side_effects=True, vmem_limit_bytes=60 * 1024 * 1024
        ),
    )(time_start, q, kv, go)
    return out[:, None]


def solution(mesh):
    sizes = (mesh.shape["section"], mesh.shape["ha"], mesh.shape["wa"])
    return jax.shard_map(
        functools.partial(local, sizes),
        mesh=mesh,
        in_specs=(
            P("section", None, "ha", "wa", None, None),
            P(None, "section", None, "ha", "wa", None, None),
            P("section", None, "ha", "wa", None, None),
            P(None, "ha", "wa"),
        ),
        out_specs=P(None, "section", None, "ha", "wa", None, None),
        check_vma=False,
    )
```

```python
import functools

import jax
import jax.numpy as jnp
from jax import lax
from jax.experimental import pallas as pl
from jax.experimental.pallas import tpu as pltpu
from jax.sharding import PartitionSpec as P

HEAD_DIM = 128
HEADS_PER_CHUNK = 2
MESH = pl.DeviceIdType.MESH
F32 = jnp.float32
BF16 = jnp.bfloat16

Y_KV, Z_KV, CORNER, Z_PART, Y_PART, OUT_Q, OUT_KV, CORNER_PART, KINDS = 0, 1, 3, 5, 7, 8, 9, 10, 12

AHEAD = 2
CORNERS_AHEAD = 1


def wa_first(c):
    return lax.rem(c, 3) == 2


def dot(a, b, contract):
    return lax.dot_general(a, b, ((contract[0], contract[1]), ((), ())), preferred_element_type=F32)


def kernel(sizes, starts, q_in, kv_in, go_in, out, q, kv, go, load_sem, hy, hz, pz_send, pz_recv, py_send, py_recv,
           acc, acc_y, dq, dkv, bias, send_sem, recv_sem):
    n_sec, n_ha, n_wa, chunks, width = sizes
    grid_t, rows, cols, tok, _ = q.shape
    sec, ha, wa = lax.axis_index("section"), lax.axis_index("ha"), lax.axis_index("wa")
    before = lax.rem(sec + n_sec - 1, n_sec)
    after = lax.rem(sec + 1, n_sec)
    other = 1 - ha
    edge = other * (rows - 1)
    has = (wa > 0, wa < n_wa - 1)
    peer = (wa - 1, wa + 1)
    near = (0, cols - 1)
    scale = HEAD_DIM ** (-0.5)

    loads = [pltpu.make_async_copy(src, dst, load_sem.at[n])
             for n, (src, dst) in enumerate(((q_in, q), (kv_in, kv), (go_in, go)))]
    barrier = pltpu.get_barrier_semaphore()
    pl.semaphore_signal(barrier, inc=1, device_id=(before, ha, wa), device_id_type=MESH)
    pl.semaphore_signal(barrier, inc=1, device_id=(after, ha, wa), device_id_type=MESH)
    pl.semaphore_signal(barrier, inc=1, device_id=(sec, other, wa), device_id_type=MESH)
    for side in (0, 1):
        @pl.when(has[side])
        def _():
            pl.semaphore_signal(barrier, inc=1, device_id=(sec, ha, peer[side]), device_id_type=MESH)
    pl.semaphore_wait(barrier, 3 + jnp.minimum(wa, 1) + jnp.minimum(n_wa - 1 - wa, 1))

    def lanes(c):
        return pl.ds(pl.multiple_of(c * width, width), width)

    def remote(src, dst, sent, arrived, c, device):
        return pltpu.make_async_remote_copy(
            src_ref=src, dst_ref=dst, send_sem=send_sem.at[sent, c], recv_sem=recv_sem.at[arrived, c],
            device_id=device, device_id_type=MESH)

    def y_kv(c):
        return remote(kv_in.at[:, :, edge, :, :, lanes(c)], hy.at[:, :, :, :, lanes(c)],
                      Y_KV, Y_KV, c, (sec, other, wa))

    def z_kv(side, c):
        return remote(kv_in.at[:, :, :, near[side], :, lanes(c)], hz.at[1 - side, :, :, 0:rows, :, lanes(c)],
                      Z_KV + side, Z_KV + 1 - side, c, (sec, ha, peer[side]))

    def z_corner(side, c):
        return remote(hy.at[:, :, near[side], :, lanes(c)], hz.at[1 - side, :, :, rows, :, lanes(c)],
                      CORNER + side, CORNER + 1 - side, c, (sec, ha, peer[side]))

    def y_corner(side, c):
        return remote(hz.at[side, :, :, edge, :, lanes(c)], hz.at[side, :, :, rows, :, lanes(c)],
                      CORNER + side, CORNER + side, c, (sec, other, wa))

    def z_part(side, c, count):
        return remote(pz_send.at[side, :, :, 0:count, :, lanes(c)], pz_recv.at[1 - side, :, :, 0:count, :, lanes(c)],
                      Z_PART + side, Z_PART + 1 - side, c, (sec, ha, peer[side]))

    def corner_part(side, c):
        return remote(pz_send.at[side, :, :, rows, :, lanes(c)], pz_recv.at[side, :, :, rows, :, lanes(c)],
                      CORNER_PART + side, CORNER_PART + side, c, (sec, other, wa))

    def y_part(c):
        return remote(py_send.at[:, :, :, :, lanes(c)], py_recv.at[:, :, :, :, lanes(c)],
                      Y_PART, Y_PART, c, (sec, other, wa))

    def out_q(c):
        return remote(dq.at[:, :, :, :, lanes(c)], out.at[0, :, :, :, :, lanes(c)],
                      OUT_Q, OUT_Q, c, (before, ha, wa))

    def out_kv(c):
        return remote(dkv.at[:, :, :, :, :, lanes(c)], out.at[pl.ds(1, 2), :, :, :, :, lanes(c)],
                      OUT_KV, OUT_KV, c, (before, ha, wa))

    n_own, n_y, n_z = grid_t * rows * cols * tok, grid_t * cols * tok, grid_t * (rows + 1) * tok
    n_q = n_own
    cut = (0, n_own, n_own + n_y, n_own + n_y + n_z, n_own + n_y + 2 * n_z)

    def stage_send(c):
        y_kv(c).start()
        for side in (0, 1):
            @pl.when(has[side])
            def _():
                z_kv(side, c).start()

    def sides(action):
        for side in (0, 1):
            @pl.when(has[side])
            def _():
                action(side)

    def stage_corner(c):
        def ha_then_wa():
            y_kv(c).wait_recv()
            sides(lambda side: z_corner(side, c).start())

        def wa_then_ha():
            def pass_on(side):
                z_kv(1 - side, c).wait_recv()
                y_corner(side, c).start()
            sides(pass_on)

        lax.cond(wa_first(c), wa_then_ha, ha_then_wa)

    def head(h):
        ch = pl.ds(pl.multiple_of(h * HEAD_DIM, HEAD_DIM), HEAD_DIM)
        qh = q[:, :, :, :, ch].reshape(n_q, HEAD_DIM)
        gh = go[:, :, :, :, ch].reshape(n_q, HEAD_DIM)

        def gather(i):
            return jnp.concatenate([
                kv[i, :, :, :, :, ch].reshape(n_own, HEAD_DIM), hy[i, :, :, :, ch].reshape(n_y, HEAD_DIM),
                hz[0, i, :, :, :, ch].reshape(n_z, HEAD_DIM), hz[1, i, :, :, :, ch].reshape(n_z, HEAD_DIM)])

        k, v = gather(0), gather(1)
        s = dot(k, qh, ((1,), (1,))) * scale + bias[...]
        e = jnp.exp(s - jnp.max(s, axis=0, keepdims=True))
        p = e * (1.0 / jnp.sum(e, axis=0, keepdims=True))
        dp = dot(v, gh, ((1,), (1,)))
        delta = jnp.sum(p * dp, axis=0, keepdims=True)
        ds = (p * (dp - delta)).astype(BF16)
        grads = (dot(ds, qh, ((1,), (0,))) * scale, dot(p.astype(BF16), gh, ((1,), (0,))))
        q_grad = dot(ds, k, ((0,), (0,))) * scale
        dq[:, :, :, :, ch] = q_grad.astype(BF16).reshape(grid_t, rows, cols, tok, HEAD_DIM)
        for i in (0, 1):
            acc[i, :, :, :, :, ch] = grads[i][cut[0]:cut[1]].reshape(grid_t, rows, cols, tok, HEAD_DIM)
            acc_y[i, :, :, :, ch] = grads[i][cut[1]:cut[2]].reshape(grid_t, cols, tok, HEAD_DIM)
            for side in (0, 1):
                part = grads[i][cut[2 + side]:cut[3 + side]].astype(BF16)
                pz_send[side, i, :, :, :, ch] = part.reshape(grid_t, rows + 1, tok, HEAD_DIM)

    def stage_compute(c):
        def ha_then_wa():
            def arrive(side):
                z_kv(1 - side, c).wait_recv()
                z_corner(1 - side, c).wait_recv()
            sides(arrive)

        def wa_then_ha():
            y_kv(c).wait_recv()
            sides(lambda side: y_corner(side, c).wait_recv())

        lax.cond(wa_first(c), wa_then_ha, ha_then_wa)
        for j in range(HEADS_PER_CHUNK):
            head(c * HEADS_PER_CHUNK + j)

        def send_ha_then_wa():
            sides(lambda side: z_part(side, c, rows + 1).start())

        def send_wa_then_ha():
            py_send[:, :, :, :, lanes(c)] = acc_y[:, :, :, :, lanes(c)].astype(BF16)
            y_part(c).start()
            sides(lambda side: corner_part(side, c).start())

        lax.cond(wa_first(c), send_wa_then_ha, send_ha_then_wa)
        out_q(c).start()

    def stage_fold(c):
        ch = lanes(c)

        def ha_then_wa():
            def fold(side):
                z_part(1 - side, c, rows + 1).wait_recv()
                for i in (0, 1):
                    acc[i, :, :, near[side], :, ch] += pz_recv[side, i, :, 0:rows, :, ch].astype(F32)
                    acc_y[i, :, near[side], :, ch] += pz_recv[side, i, :, rows, :, ch].astype(F32)
            sides(fold)
            py_send[:, :, :, :, ch] = acc_y[:, :, :, :, ch].astype(BF16)
            y_part(c).start()

        def wa_then_ha():
            def fold(side):
                corner_part(side, c).wait_recv()
                for i in (0, 1):
                    pz_send[side, i, :, edge, :, ch] = (
                        pz_send[side, i, :, edge, :, ch].astype(F32) + pz_recv[side, i, :, rows, :, ch].astype(F32)
                    ).astype(BF16)
                z_part(side, c, rows).start()
            sides(fold)

        lax.cond(wa_first(c), wa_then_ha, ha_then_wa)

    def stage_out(c):
        ch = lanes(c)
        y_part(c).wait_recv()
        acc[:, :, edge, :, :, ch] += py_recv[:, :, :, :, ch].astype(F32)

        @pl.when(wa_first(c))
        def _():
            def fold(side):
                z_part(1 - side, c, rows).wait_recv()
                for i in (0, 1):
                    acc[i, :, :, near[side], :, ch] += pz_recv[side, i, :, 0:rows, :, ch].astype(F32)
            sides(fold)

        dkv[:, :, :, :, :, ch] = acc[:, :, :, :, :, ch].astype(BF16)
        out_kv(c).start()

    for c in range(AHEAD):
        stage_send(c)
    for load in loads:
        load.start()

    lane = lax.broadcasted_iota(jnp.int32, (1, n_q), 1)
    first = jnp.zeros((1, n_q), jnp.int32)
    for t in range(grid_t):
        for r in range(rows):
            for c in range(cols):
                tile = (t * rows + r) * cols + c
                first = jnp.where(lane // tok == tile, starts[r, c, t], first)
    col = (lane // tok) % cols
    low_first, high_last = wa == 0, wa == n_wa - 1
    in_left = jnp.where(low_first, 0, jnp.where(high_last, 1, (col == 0).astype(jnp.int32)))
    in_right = jnp.where(high_last, 0, jnp.where(low_first, 1, (col == cols - 1).astype(jnp.int32)))
    always = jnp.ones((1, n_q), jnp.int32)
    for at, per_t, inside in ((0, rows * cols * tok, always), (1, cols * tok, always),
                              (2, (rows + 1) * tok, in_left), (3, (rows + 1) * tok, in_right)):
        for t in range(grid_t):
            seen = (first <= t) & (first + 2 >= t) & (inside > 0)
            row = jnp.where(seen, 0.0, -1e30).astype(F32)
            bias[cut[at] + t * per_t:cut[at] + (t + 1) * per_t, :] = jnp.broadcast_to(row, (per_t, n_q))
    for side in (0, 1):
        @pl.when(jnp.logical_not(has[side]))
        def _():
            hz[side] = jnp.zeros(hz.shape[1:], BF16)

    def step(i, carry):
        @pl.when(i + AHEAD < chunks)
        def _():
            stage_send(i + AHEAD)

        @pl.when(i + CORNERS_AHEAD < chunks)
        def _():
            stage_corner(i + CORNERS_AHEAD)

        @pl.when(i < chunks)
        def _():
            stage_compute(i)

        @pl.when((i >= 1) & (i < chunks + 1))
        def _():
            stage_fold(i - 1)

        @pl.when(i >= 2)
        def _():
            stage_out(i - 2)
        return carry

    for c in range(CORNERS_AHEAD):
        stage_corner(c)
    for load in loads:
        load.wait()
    lax.fori_loop(0, chunks + 2, step, 0)

    def finish(c, carry):
        y_kv(c).wait_send()
        y_part(c).wait_send()
        sides(lambda side: z_kv(side, c).wait_send())

        def ha_then_wa():
            def sent(side):
                z_corner(side, c).wait_send()
                z_part(side, c, rows + 1).wait_send()
            sides(sent)

        def wa_then_ha():
            def sent(side):
                y_corner(side, c).wait_send()
                corner_part(side, c).wait_send()
                z_part(side, c, rows).wait_send()
            sides(sent)

        lax.cond(wa_first(c), wa_then_ha, ha_then_wa)
        out_q(c).wait()
        out_kv(c).wait()
        return carry

    lax.fori_loop(0, chunks, finish, 0)


def local(mesh_sizes, queries, keys_values, grad_out, time_start):
    n_sec, n_ha, n_wa = mesh_sizes
    q, kv, go = queries[0], keys_values[:, 0], grad_out[0]
    grid_t, rows, cols, tok, channels = q.shape
    assert n_ha == 2 and rows == 2 and cols == 2 and n_wa >= 2 and n_sec >= 2
    width = HEADS_PER_CHUNK * HEAD_DIM
    assert channels % width == 0
    chunks = channels // width
    assert chunks >= AHEAD >= CORNERS_AHEAD
    n_q = grid_t * rows * cols * tok
    n_k = n_q + grid_t * tok * (cols + 2 * (rows + 1))
    stay = pl.BlockSpec(memory_space=pl.ANY)
    out = pl.pallas_call(
        functools.partial(kernel, (n_sec, n_ha, n_wa, chunks, width)),
        out_shape=jax.ShapeDtypeStruct((3,) + q.shape, BF16),
        in_specs=[pl.BlockSpec(memory_space=pltpu.SMEM), stay, stay, stay],
        out_specs=pl.BlockSpec(memory_space=pl.ANY),
        scratch_shapes=[
            pltpu.VMEM(q.shape, BF16),
            pltpu.VMEM(kv.shape, BF16),
            pltpu.VMEM(go.shape, BF16),
            pltpu.SemaphoreType.DMA((3,)),
            pltpu.VMEM((2, grid_t, cols, tok, channels), BF16),
            pltpu.VMEM((2, 2, grid_t, rows + 1, tok, channels), BF16),
            pltpu.VMEM((2, 2, grid_t, rows + 1, tok, channels), BF16),
            pltpu.VMEM((2, 2, grid_t, rows + 1, tok, channels), BF16),
            pltpu.VMEM((2, grid_t, cols, tok, channels), BF16),
            pltpu.VMEM((2, grid_t, cols, tok, channels), BF16),
            pltpu.VMEM((2,) + q.shape, F32),
            pltpu.VMEM((2, grid_t, cols, tok, channels), F32),
            pltpu.VMEM(q.shape, BF16),
            pltpu.VMEM((2,) + q.shape, BF16),
            pltpu.VMEM((n_k, n_q), F32),
            pltpu.SemaphoreType.DMA((KINDS, chunks)),
            pltpu.SemaphoreType.DMA((KINDS, chunks)),
        ],
        compiler_params=pltpu.CompilerParams(
            collective_id=0, has_side_effects=True, vmem_limit_bytes=60 * 1024 * 1024
        ),
    )(time_start.transpose(1, 2, 0), q, kv, go)
    return out[:, None]


def solution(mesh):
    sizes = (mesh.shape["section"], mesh.shape["ha"], mesh.shape["wa"])
    return jax.shard_map(
        functools.partial(local, sizes),
        mesh=mesh,
        in_specs=(
            P("section", None, "ha", "wa", None, None),
            P(None, "section", None, "ha", "wa", None, None),
            P("section", None, "ha", "wa", None, None),
            P(None, "ha", "wa"),
        ),
        out_specs=P(None, "section", None, "ha", "wa", None, None),
        check_vma=False,
    )
```

```python
import functools

import jax
import jax.numpy as jnp
from jax import lax
from jax.experimental import pallas as pl
from jax.experimental.pallas import tpu as pltpu
from jax.sharding import PartitionSpec as P

HEAD_DIM = 128
HEADS_PER_CHUNK = 1
MESH = pl.DeviceIdType.MESH
F32 = jnp.float32
BF16 = jnp.bfloat16

Y_KV, Z_KV, CORNER, Z_PART, Y_PART, OUT_Q, OUT_KV, CORNER_PART, KINDS = 0, 1, 3, 5, 7, 8, 9, 10, 12

AHEAD = 5
CORNERS_AHEAD = 3
FOLD_LAG = 3
OUT_LAG = 6


def wa_first(c):
    return lax.rem(c, 3) == 1


def dot(a, b, contract):
    return lax.dot_general(a, b, ((contract[0], contract[1]), ((), ())), preferred_element_type=F32)


def kernel(sizes, starts, q_in, kv_in, go_in, out, q, kv, go, load_sem, hy, hz, pz_send, pz_recv, py_send, py_recv,
           acc, acc_y, dq, dkv, bias, send_sem, recv_sem):
    n_sec, n_ha, n_wa, chunks, width = sizes
    grid_t, rows, cols, tok, _ = q.shape
    sec, ha, wa = lax.axis_index("section"), lax.axis_index("ha"), lax.axis_index("wa")
    before = lax.rem(sec + n_sec - 1, n_sec)
    after = lax.rem(sec + 1, n_sec)
    other = 1 - ha
    edge = other * (rows - 1)
    has = (wa > 0, wa < n_wa - 1)
    peer = (wa - 1, wa + 1)
    near = (0, cols - 1)
    scale = HEAD_DIM ** (-0.5)

    loads = [pltpu.make_async_copy(src, dst, load_sem.at[n])
             for n, (src, dst) in enumerate(((q_in, q), (kv_in, kv), (go_in, go)))]
    barrier = pltpu.get_barrier_semaphore()
    pl.semaphore_signal(barrier, inc=1, device_id=(before, ha, wa), device_id_type=MESH)
    pl.semaphore_signal(barrier, inc=1, device_id=(after, ha, wa), device_id_type=MESH)
    pl.semaphore_signal(barrier, inc=1, device_id=(sec, other, wa), device_id_type=MESH)
    for side in (0, 1):
        @pl.when(has[side])
        def _():
            pl.semaphore_signal(barrier, inc=1, device_id=(sec, ha, peer[side]), device_id_type=MESH)
    pl.semaphore_wait(barrier, 3 + jnp.minimum(wa, 1) + jnp.minimum(n_wa - 1 - wa, 1))

    def lanes(c):
        return pl.ds(pl.multiple_of(c * width, width), width)

    def remote(src, dst, sent, arrived, c, device):
        return pltpu.make_async_remote_copy(
            src_ref=src, dst_ref=dst, send_sem=send_sem.at[sent, c], recv_sem=recv_sem.at[arrived, c],
            device_id=device, device_id_type=MESH)

    def y_kv(c):
        return remote(kv_in.at[:, :, edge, :, :, lanes(c)], hy.at[:, :, :, :, lanes(c)],
                      Y_KV, Y_KV, c, (sec, other, wa))

    def z_kv(side, c):
        return remote(kv_in.at[:, :, :, near[side], :, lanes(c)], hz.at[1 - side, :, :, 0:rows, :, lanes(c)],
                      Z_KV + side, Z_KV + 1 - side, c, (sec, ha, peer[side]))

    def z_corner(side, c):
        return remote(hy.at[:, :, near[side], :, lanes(c)], hz.at[1 - side, :, :, rows, :, lanes(c)],
                      CORNER + side, CORNER + 1 - side, c, (sec, ha, peer[side]))

    def y_corner(side, c):
        return remote(hz.at[side, :, :, edge, :, lanes(c)], hz.at[side, :, :, rows, :, lanes(c)],
                      CORNER + side, CORNER + side, c, (sec, other, wa))

    def z_part(side, c, count):
        return remote(pz_send.at[side, :, :, 0:count, :, lanes(c)], pz_recv.at[1 - side, :, :, 0:count, :, lanes(c)],
                      Z_PART + side, Z_PART + 1 - side, c, (sec, ha, peer[side]))

    def corner_part(side, c):
        return remote(pz_send.at[side, :, :, rows, :, lanes(c)], pz_recv.at[side, :, :, rows, :, lanes(c)],
                      CORNER_PART + side, CORNER_PART + side, c, (sec, other, wa))

    def y_part(c):
        return remote(py_send.at[:, :, :, :, lanes(c)], py_recv.at[:, :, :, :, lanes(c)],
                      Y_PART, Y_PART, c, (sec, other, wa))

    def out_q(c):
        return remote(dq.at[:, :, :, :, lanes(c)], out.at[0, :, :, :, :, lanes(c)],
                      OUT_Q, OUT_Q, c, (before, ha, wa))

    def out_kv(c):
        return remote(dkv.at[:, :, :, :, :, lanes(c)], out.at[pl.ds(1, 2), :, :, :, :, lanes(c)],
                      OUT_KV, OUT_KV, c, (before, ha, wa))

    n_own, n_y, n_z = grid_t * rows * cols * tok, grid_t * cols * tok, grid_t * (rows + 1) * tok
    n_q = n_own
    cut = (0, n_own, n_own + n_y, n_own + n_y + n_z, n_own + n_y + 2 * n_z)

    def stage_send(c):
        y_kv(c).start()
        for side in (0, 1):
            @pl.when(has[side])
            def _():
                z_kv(side, c).start()

    def sides(action):
        for side in (0, 1):
            @pl.when(has[side])
            def _():
                action(side)

    def stage_corner(c):
        def ha_then_wa():
            y_kv(c).wait_recv()
            sides(lambda side: z_corner(side, c).start())

        def wa_then_ha():
            def pass_on(side):
                z_kv(1 - side, c).wait_recv()
                y_corner(side, c).start()
            sides(pass_on)

        lax.cond(wa_first(c), wa_then_ha, ha_then_wa)

    def head(h):
        ch = pl.ds(pl.multiple_of(h * HEAD_DIM, HEAD_DIM), HEAD_DIM)
        qh = q[:, :, :, :, ch].reshape(n_q, HEAD_DIM)
        gh = go[:, :, :, :, ch].reshape(n_q, HEAD_DIM)

        def gather(i):
            return jnp.concatenate([
                kv[i, :, :, :, :, ch].reshape(n_own, HEAD_DIM), hy[i, :, :, :, ch].reshape(n_y, HEAD_DIM),
                hz[0, i, :, :, :, ch].reshape(n_z, HEAD_DIM), hz[1, i, :, :, :, ch].reshape(n_z, HEAD_DIM)])

        k, v = gather(0), gather(1)
        s = dot(k, qh, ((1,), (1,))) * scale + bias[...]
        e = jnp.exp(s - jnp.max(s, axis=0, keepdims=True))
        p = e * (1.0 / jnp.sum(e, axis=0, keepdims=True))
        dp = dot(v, gh, ((1,), (1,)))
        delta = jnp.sum(p * dp, axis=0, keepdims=True)
        ds = (p * (dp - delta)).astype(BF16)
        grads = (dot(ds, qh, ((1,), (0,))) * scale, dot(p.astype(BF16), gh, ((1,), (0,))))
        q_grad = dot(ds, k, ((0,), (0,))) * scale
        dq[:, :, :, :, ch] = q_grad.astype(BF16).reshape(grid_t, rows, cols, tok, HEAD_DIM)
        for i in (0, 1):
            acc[i, :, :, :, :, ch] = grads[i][cut[0]:cut[1]].reshape(grid_t, rows, cols, tok, HEAD_DIM)
            acc_y[i, :, :, :, ch] = grads[i][cut[1]:cut[2]].reshape(grid_t, cols, tok, HEAD_DIM)
            for side in (0, 1):
                part = grads[i][cut[2 + side]:cut[3 + side]].astype(BF16)
                pz_send[side, i, :, :, :, ch] = part.reshape(grid_t, rows + 1, tok, HEAD_DIM)

    def stage_compute(c):
        def ha_then_wa():
            def arrive(side):
                z_kv(1 - side, c).wait_recv()
                z_corner(1 - side, c).wait_recv()
            sides(arrive)

        def wa_then_ha():
            y_kv(c).wait_recv()
            sides(lambda side: y_corner(side, c).wait_recv())

        lax.cond(wa_first(c), wa_then_ha, ha_then_wa)
        for j in range(HEADS_PER_CHUNK):
            head(c * HEADS_PER_CHUNK + j)

        def send_ha_then_wa():
            sides(lambda side: z_part(side, c, rows + 1).start())

        def send_wa_then_ha():
            py_send[:, :, :, :, lanes(c)] = acc_y[:, :, :, :, lanes(c)].astype(BF16)
            y_part(c).start()
            sides(lambda side: corner_part(side, c).start())

        lax.cond(wa_first(c), send_wa_then_ha, send_ha_then_wa)
        out_q(c).start()

    def stage_fold(c):
        ch = lanes(c)

        def ha_then_wa():
            def fold(side):
                z_part(1 - side, c, rows + 1).wait_recv()
                for i in (0, 1):
                    acc[i, :, :, near[side], :, ch] += pz_recv[side, i, :, 0:rows, :, ch].astype(F32)
                    acc_y[i, :, near[side], :, ch] += pz_recv[side, i, :, rows, :, ch].astype(F32)
            sides(fold)
            py_send[:, :, :, :, ch] = acc_y[:, :, :, :, ch].astype(BF16)
            y_part(c).start()

        def wa_then_ha():
            def fold(side):
                corner_part(side, c).wait_recv()
                for i in (0, 1):
                    pz_send[side, i, :, edge, :, ch] = (
                        pz_send[side, i, :, edge, :, ch].astype(F32) + pz_recv[side, i, :, rows, :, ch].astype(F32)
                    ).astype(BF16)
                z_part(side, c, rows).start()
            sides(fold)

        lax.cond(wa_first(c), wa_then_ha, ha_then_wa)

    def stage_out(c):
        ch = lanes(c)
        y_part(c).wait_recv()
        acc[:, :, edge, :, :, ch] += py_recv[:, :, :, :, ch].astype(F32)

        @pl.when(wa_first(c))
        def _():
            def fold(side):
                z_part(1 - side, c, rows).wait_recv()
                for i in (0, 1):
                    acc[i, :, :, near[side], :, ch] += pz_recv[side, i, :, 0:rows, :, ch].astype(F32)
            sides(fold)

        dkv[:, :, :, :, :, ch] = acc[:, :, :, :, :, ch].astype(BF16)
        out_kv(c).start()

    for c in range(AHEAD):
        stage_send(c)
    for load in loads:
        load.start()

    lane = lax.broadcasted_iota(jnp.int32, (1, n_q), 1)
    first = jnp.zeros((1, n_q), jnp.int32)
    for t in range(grid_t):
        for r in range(rows):
            for c in range(cols):
                tile = (t * rows + r) * cols + c
                first = jnp.where(lane // tok == tile, starts[r, c, t], first)
    col = (lane // tok) % cols
    low_first, high_last = wa == 0, wa == n_wa - 1
    in_left = jnp.where(low_first, 0, jnp.where(high_last, 1, (col == 0).astype(jnp.int32)))
    in_right = jnp.where(high_last, 0, jnp.where(low_first, 1, (col == cols - 1).astype(jnp.int32)))
    always = jnp.ones((1, n_q), jnp.int32)
    for at, per_t, inside in ((0, rows * cols * tok, always), (1, cols * tok, always),
                              (2, (rows + 1) * tok, in_left), (3, (rows + 1) * tok, in_right)):
        for t in range(grid_t):
            seen = (first <= t) & (first + 2 >= t) & (inside > 0)
            row = jnp.where(seen, 0.0, -1e30).astype(F32)
            bias[cut[at] + t * per_t:cut[at] + (t + 1) * per_t, :] = jnp.broadcast_to(row, (per_t, n_q))
    for side in (0, 1):
        @pl.when(jnp.logical_not(has[side]))
        def _():
            hz[side] = jnp.zeros(hz.shape[1:], BF16)

    def step(i, carry):
        @pl.when(i + AHEAD < chunks)
        def _():
            stage_send(i + AHEAD)

        @pl.when(i + CORNERS_AHEAD < chunks)
        def _():
            stage_corner(i + CORNERS_AHEAD)

        @pl.when(i < chunks)
        def _():
            stage_compute(i)

        @pl.when((i >= FOLD_LAG) & (i < chunks + FOLD_LAG))
        def _():
            stage_fold(i - FOLD_LAG)

        @pl.when(i >= OUT_LAG)
        def _():
            stage_out(i - OUT_LAG)
        return carry

    for c in range(CORNERS_AHEAD):
        stage_corner(c)
    for load in loads:
        load.wait()
    lax.fori_loop(0, chunks + OUT_LAG, step, 0)

    def finish(c, carry):
        y_kv(c).wait_send()
        y_part(c).wait_send()
        sides(lambda side: z_kv(side, c).wait_send())

        def ha_then_wa():
            def sent(side):
                z_corner(side, c).wait_send()
                z_part(side, c, rows + 1).wait_send()
            sides(sent)

        def wa_then_ha():
            def sent(side):
                y_corner(side, c).wait_send()
                corner_part(side, c).wait_send()
                z_part(side, c, rows).wait_send()
            sides(sent)

        lax.cond(wa_first(c), wa_then_ha, ha_then_wa)
        out_q(c).wait()
        out_kv(c).wait()
        return carry

    lax.fori_loop(0, chunks, finish, 0)


def copy_kernel(src, dst, held, sems):
    parts = [(i, t) for i in range(src.shape[0]) for t in range(src.shape[1])]
    come = [pltpu.make_async_copy(src.at[p], held.at[p], sems.at[0, n]) for n, p in enumerate(parts)]
    go = [pltpu.make_async_copy(held.at[p], dst.at[p], sems.at[1, n]) for n, p in enumerate(parts)]
    for copy in come:
        copy.start()
    for a, b in zip(come, go):
        a.wait()
        b.start()
    for copy in go:
        copy.wait()


def local(mesh_sizes, queries, keys_values, grad_out, time_start):
    n_sec, n_ha, n_wa = mesh_sizes
    q, kv, go = queries[0], keys_values[:, 0], grad_out[0]
    grid_t, rows, cols, tok, channels = q.shape
    assert n_ha == 2 and rows == 2 and cols == 2 and n_wa >= 2 and n_sec >= 2
    width = HEADS_PER_CHUNK * HEAD_DIM
    assert channels % width == 0
    chunks = channels // width
    assert chunks >= AHEAD >= CORNERS_AHEAD
    n_q = grid_t * rows * cols * tok
    n_k = n_q + grid_t * tok * (cols + 2 * (rows + 1))
    stay = pl.BlockSpec(memory_space=pl.ANY)
    out = pl.pallas_call(
        functools.partial(kernel, (n_sec, n_ha, n_wa, chunks, width)),
        out_shape=jax.ShapeDtypeStruct((3,) + q.shape, BF16),
        in_specs=[pl.BlockSpec(memory_space=pltpu.SMEM), stay, stay, stay],
        out_specs=pl.BlockSpec(memory_space=pl.ANY),
        scratch_shapes=[
            pltpu.VMEM(q.shape, BF16),
            pltpu.VMEM(kv.shape, BF16),
            pltpu.VMEM(go.shape, BF16),
            pltpu.SemaphoreType.DMA((3,)),
            pltpu.VMEM((2, grid_t, cols, tok, channels), BF16),
            pltpu.VMEM((2, 2, grid_t, rows + 1, tok, channels), BF16),
            pltpu.VMEM((2, 2, grid_t, rows + 1, tok, channels), BF16),
            pltpu.VMEM((2, 2, grid_t, rows + 1, tok, channels), BF16),
            pltpu.VMEM((2, grid_t, cols, tok, channels), BF16),
            pltpu.VMEM((2, grid_t, cols, tok, channels), BF16),
            pltpu.VMEM((2,) + q.shape, F32),
            pltpu.VMEM((2, grid_t, cols, tok, channels), F32),
            pltpu.VMEM(q.shape, BF16),
            pltpu.VMEM((2,) + q.shape, BF16),
            pltpu.VMEM((n_k, n_q), F32),
            pltpu.SemaphoreType.DMA((KINDS, chunks)),
            pltpu.SemaphoreType.DMA((KINDS, chunks)),
        ],
        compiler_params=pltpu.CompilerParams(
            collective_id=0, has_side_effects=True, vmem_limit_bytes=60 * 1024 * 1024
        ),
    )(time_start.transpose(1, 2, 0), q, kv, go)
    out = pl.pallas_call(
        copy_kernel,
        out_shape=jax.ShapeDtypeStruct(out.shape, BF16),
        in_specs=[pl.BlockSpec(memory_space=pl.ANY)],
        out_specs=pl.BlockSpec(memory_space=pl.ANY),
        scratch_shapes=[pltpu.VMEM(out.shape, BF16), pltpu.SemaphoreType.DMA((2, 3 * grid_t))],
    )(out)
    return out[:, None]


def solution(mesh):
    sizes = (mesh.shape["section"], mesh.shape["ha"], mesh.shape["wa"])
    return jax.shard_map(
        functools.partial(local, sizes),
        mesh=mesh,
        in_specs=(
            P("section", None, "ha", "wa", None, None),
            P(None, "section", None, "ha", "wa", None, None),
            P("section", None, "ha", "wa", None, None),
            P(None, "ha", "wa"),
        ),
        out_specs=P(None, "section", None, "ha", "wa", None, None),
        check_vma=False,
    )
```
